32 devices in a mesh: rep: 2 (over y), col: 4 (over z), row: 2 (over x), sub: 2 (over core).
Axes of the slice: x: 2, y: 2, z: 4, core: 2. Of those that a mesh axis runs over, the one named last changes fastest.
Arguments:
- node_query: bfloat16 [512, 256], P(('rep', 'row')), parts along dimension 0, may hold values from -6 to 6
- query_angles: float32 [3, 512], P(None, ('rep', 'row')), parts along dimension 1, may hold values from -3.140625 to 3.140625
- query_trans: float32 [3, 512], P(None, ('rep', 'row')), parts along dimension 1, may hold values from -12 to 26
- query_chain: int32 [512], P(('rep', 'row')), parts along dimension 0, may hold values from 0 to 3
- node_key: bfloat16 [2048, 256], P(('rep', 'col', 'row', 'sub')), parts along dimension 0, may hold values from -6 to 6
- key_angles: float32 [3, 2048], P(None, ('rep', 'col')), parts along dimension 1, may hold values from -3.140625 to 3.140625
- key_trans: float32 [3, 2048], P(None, ('rep', 'col')), parts along dimension 1, may hold values from -12 to 12
- key_chain: int32 [2048], P(('rep', 'col')), parts along dimension 0, may hold values from 0 to 3, never falling along the last dimension, each value on 1 to 512 neighbouring positions
- pair_features: bfloat16 [128, 512, 1024], P('sub', ('rep', 'row'), 'col'), parts along dimension 1, may hold values from -6 to 6
- pair_mask: int32 [512, 1024], P(('rep', 'row'), 'col'), parts along dimension 0, may hold values 0 or 1
- query_weight: bfloat16 [256, 336], P(None, 'sub'), may hold values from -0.375 to 0.375
- key_weight: bfloat16 [256, 816], P(None, 'sub'), may hold values from -0.375 to 0.375
- bias_weight: bfloat16 [128, 12], P(None, 'sub'), may hold values from -0.5 to 0.5
- point_gain: float32 [12], P('sub'), may hold values from 0.25 to 2
- chain_gain: float32 [12], P('sub'), may hold values from -2 to 2
- out_weight: bfloat16 [2112, 256], P('sub'), may hold values from -0.125 to 0.125
- first_gain: float32 [256], replicated, may hold values from 0.5 to 1.5
- second_gain: float32 [256], replicated, may hold values from 0.5 to 1.5
- gate_weight: bfloat16 [256, 1024], replicated, may hold values from -0.375 to 0.375
- up_weight: bfloat16 [256, 1024], replicated, may hold values from -0.375 to 0.375
- down_weight: bfloat16 [1024, 256], replicated, may hold values from -0.1875 to 0.1875
- edge_query_weight: bfloat16 [256, 256], replicated, may hold values from -0.375 to 0.375
- edge_key_weight: bfloat16 [256, 256], replicated, may hold values from -0.375 to 0.375
- edge_in_weight: bfloat16 [128, 256], replicated, may hold values from -0.5 to 0.5
- edge_out_weight: bfloat16 [256, 128], replicated, may hold values from -0.375 to 0.375
Outputs:
- updated_nodes: bfloat16 [512, 256], P(('rep', 'row')), parts along dimension 0
- updated_pairs: bfloat16 [128, 512, 1024], P('sub', ('rep', 'row'), 'col'), parts along dimension 1
The draws below stay inside these ranges and needn't reach their ends.
There are 2 independent parts, one for each index of `rep`. The reference program is written for one: setup_inputs(seed, part) draws one part's arguments, and reference() takes and returns one part's arrays. A program takes and returns all parts, laid end to end along the dimension named above; an argument that names none is the same for every part. Nothing has to cross between parts.
All inputs are finite; a program needn't handle non-finite values. No bound on the sum of `pair_mask` on one device may be relied on, other than what follows from the above.
Results may differ from the reference program's by a relative error of at most 0.006.
Values may be sent and summed in bfloat16 or wider, within the bound.
A program may use at most 128 MiB of HBM per device.

```python
import math
import jax
import jax.numpy as jnp
import numpy as np
from jax import lax

CS = 256
CZ = 128
H = 12
CH = 16
PQ = 4
PV = 8
FFN = 1024
EH = 256
NCHAIN = 4
QROWS = 256
KEYS = 1024


def draw_query_trans(key, part):
    return jnp.clip(3.0 * jax.random.normal(key, (3, QROWS), jnp.float32), -12.0, 12.0)


def plant(values, rng, low, largest):
    extent = values.shape
    spot = [jax.random.randint(jax.random.fold_in(rng, axis), (), 0, extent[axis]) for axis in range(len(extent))]
    values = values.at[tuple(spot)].set(low)
    longest = extent.index(max(extent))
    spot[longest] = (spot[longest] + 1) % extent[longest]
    return values.at[tuple(spot)].set(largest)


def levels(own_key, shape, shards, low, top_value):
    level = 1.0
    for axis_at, blocks in shards:
        heights = jax.random.uniform(jax.random.fold_in(jax.random.fold_in(own_key, 6), axis_at), (blocks,), jnp.float32, low / len(shards), top_value / len(shards))
        level = level * jnp.repeat(jnp.exp(heights), shape[axis_at] // blocks).reshape((-1,) + (1,) * (len(shape) - 1 - axis_at))
    return level


def profile(amount, total, limit, slope):
    portions = [(1 << 20) // math.isqrt(standing ** slope) + 1 for standing in range(2, amount + 1)]
    spare, holding = total - limit - (amount - 1), [1] * (amount - 1)
    while spare > 0:
        candidates = [i for i in range(amount - 1) if holding[i] < limit]
        pool, remaining = sum([portions[i] for i in candidates]), spare
        for i in candidates:
            addition = min(limit - holding[i], max(1, remaining * portions[i] // pool), spare)
            holding[i] = holding[i] + addition
            spare = spare - addition
    return np.array([limit] + holding)


def ragged_sizes(key, count, total, limit, skew):
    if count == 2:
        one = jax.random.randint(key, (), max(1, total - limit), min(limit, total - 1) + 1)
        return jnp.stack([one, total - one])
    sizes = jnp.asarray(profile(count, total, limit, skew), jnp.int32)
    pairs = (count - 1) // 2
    donor, sink = sizes[1:1 + 2 * pairs:2], sizes[2:2 + 2 * pairs:2]
    slack = jnp.minimum(donor - 1, limit - sink)
    shifted = jax.random.randint(jax.random.fold_in(key, 1), (pairs,), 0, 1 << 20) % (slack + 1)
    sizes = sizes.at[1:1 + 2 * pairs:2].set(donor - shifted).at[2:2 + 2 * pairs:2].set(sink + shifted)
    return sizes[jax.random.permutation(jax.random.fold_in(key, 2), count)]


def normal_values(rng, extent, deviation, limit, split=(), kind=jnp.bfloat16):
    result = deviation * jax.random.normal(rng, extent, jnp.float32)
    if split:
        result = result * levels(rng, extent, split, -0.22, 0.18)
    return jnp.clip(result, -limit, limit).astype(kind)


def setup_inputs(seed: int = 0, part: int = 0) -> dict:
    splits = jax.random.split(jax.random.key(seed), 26)
    own_keys = jax.random.split(jax.random.fold_in(splits[25], part), 26)
    return {
        "node_query": normal_values(own_keys[0], (QROWS, CS), 1.0, 6.0, ((0, 2),)),
        "query_angles": jnp.clip(jax.random.uniform(own_keys[1], (3, QROWS), jnp.float32, -3.140625, 3.140625), -3.140625, 3.140625),
        "query_trans": draw_query_trans(jax.random.fold_in(jax.random.fold_in(splits[25], part), 71), part),
        "query_chain": plant(jax.random.randint(own_keys[3], (QROWS,), 0, NCHAIN), jax.random.fold_in(own_keys[3], 1), 0, NCHAIN - 1).astype(jnp.int32),
        "node_key": normal_values(own_keys[4], (KEYS, CS), 1.0, 6.0, ((0, 16),)),
        "key_angles": jnp.clip(jax.random.uniform(own_keys[5], (3, KEYS), jnp.float32, -3.140625, 3.140625), -3.140625, 3.140625),
        "key_trans": normal_values(own_keys[6], (3, KEYS), 3.0, 12.0, ((1, 4),), jnp.float32),
        "key_chain": jnp.searchsorted(jnp.cumsum(ragged_sizes(own_keys[7], NCHAIN, KEYS, KEYS // 2, 0)), jnp.arange(KEYS), side="right").astype(jnp.int32),
        "pair_features": normal_values(own_keys[8], (CZ, QROWS, KEYS), 1.0, 6.0, ((0, 2), (1, 2), (2, 4))),
        "pair_mask": plant((jax.random.randint(own_keys[9], (QROWS, KEYS), 0, 8) < 7).astype(jnp.int32), jax.random.fold_in(own_keys[9], 1), 0, 1),
        "query_weight": normal_values(splits[10], (CS, H * (CH + 3 * PQ)), CS ** -0.5, 0.375, ((1, 2),)),
        "key_weight": normal_values(splits[11], (CS, H * (2 * CH + 3 * PQ + 3 * PV)), CS ** -0.5, 0.375, ((1, 2),)),
        "bias_weight": normal_values(splits[12], (CZ, H), CZ ** -0.5, 0.5, ((1, 2),)),
        "point_gain": jnp.clip(jnp.exp(math.log(2.0) - 2.0794415 * jax.random.uniform(splits[13], (H,), jnp.float32) ** levels(splits[13], (H,), ((0, 2),), -0.2, 0.2)), 0.25, 2.0),
        "chain_gain": jnp.clip(jax.random.uniform(splits[14], (H,), jnp.float32, -2.0, 2.0) * levels(splits[14], (H,), ((0, 2),), -0.4, 0.0), -2.0, 2.0),
        "out_weight": normal_values(splits[15], (H * (CH + 4 * PV + CZ), CS), (H * (CH + 4 * PV + CZ)) ** -0.5, 0.125, ((0, 2),)),
        "first_gain": jnp.clip(1.0 + 0.1 * jax.random.normal(splits[16], (CS,), jnp.float32), 0.5, 1.5),
        "second_gain": jnp.clip(1.0 + 0.1 * jax.random.normal(splits[17], (CS,), jnp.float32), 0.5, 1.5),
        "gate_weight": normal_values(splits[18], (CS, FFN), CS ** -0.5, 0.375),
        "up_weight": normal_values(splits[19], (CS, FFN), CS ** -0.5, 0.375),
        "down_weight": normal_values(splits[20], (FFN, CS), FFN ** -0.5, 0.1875),
        "edge_query_weight": normal_values(splits[21], (CS, EH), CS ** -0.5, 0.375),
        "edge_key_weight": normal_values(splits[22], (CS, EH), CS ** -0.5, 0.375),
        "edge_in_weight": normal_values(splits[23], (CZ, EH), CZ ** -0.5, 0.5),
        "edge_out_weight": normal_values(splits[24], (EH, CZ), EH ** -0.5, 0.375),
    }


linear_scale = math.sqrt(1.0 / 3.0)
masked_score = -1000000000.0
norm_epsilon = 1e-05

def exact_dot(left, right):
    return jnp.dot(left.astype(jnp.float32), right.astype(jnp.float32), precision=lax.Precision.HIGHEST)

def rotations(angles):
    cos_yaw = jnp.cos(angles[0])
    sin_yaw = jnp.sin(angles[0])
    cos_pitch = jnp.cos(angles[1])
    sin_pitch = jnp.sin(angles[1])
    cos_roll = jnp.cos(angles[2])
    sin_roll = jnp.sin(angles[2])
    first_row = jnp.stack([cos_yaw * cos_pitch, cos_yaw * sin_pitch * sin_roll - sin_yaw * cos_roll, cos_yaw * sin_pitch * cos_roll + sin_yaw * sin_roll], 0)
    second_row = jnp.stack([sin_yaw * cos_pitch, sin_yaw * sin_pitch * sin_roll + cos_yaw * cos_roll, sin_yaw * sin_pitch * cos_roll - cos_yaw * sin_roll], 0)
    third_row = jnp.stack([-sin_pitch, cos_pitch * sin_roll, cos_pitch * cos_roll], 0)
    return jnp.stack([first_row, second_row, third_row], 0)

def layer_norm(values, gain):
    centred = values - lax.optimization_barrier(jnp.mean(values, axis=-1, keepdims=True))
    variance = lax.optimization_barrier(jnp.mean(centred * centred, axis=-1, keepdims=True))
    return centred * lax.rsqrt(variance + norm_epsilon) * gain

def rounded_copy(values):
    return lax.optimization_barrier(values.astype(jnp.bfloat16)).astype(jnp.float32)

def finish_nodes(attended, node_rows, angle_rows, trans_rows, out_weight, first_gain, second_gain, gate_weight, up_weight, down_weight):
    row_count, heads = (attended.shape[0], attended.shape[1])
    global_points = attended[:, :, CH:CH + 3 * PV].reshape(row_count, heads, 3, PV) - trans_rows.T[:, None, :, None]
    local_points = jnp.einsum('bai,ihbp->ihap', rotations(angle_rows), global_points, precision=lax.Precision.HIGHEST)
    point_norms = jnp.sqrt(1.0 + lax.optimization_barrier(jnp.sum(local_points * local_points, axis=2)))
    features = jnp.concatenate([attended[:, :, :CH], local_points.reshape(row_count, heads, 3 * PV), point_norms, attended[:, :, CH + 3 * PV:]], axis=2)
    features = features.reshape(row_count, heads * features.shape[2]).astype(jnp.bfloat16)
    projected = exact_dot(features, out_weight)
    first_nodes = layer_norm(node_rows.astype(jnp.float32) + projected, first_gain)
    first_rounded = first_nodes.astype(jnp.bfloat16)
    gate = exact_dot(first_rounded, gate_weight)
    upward = exact_dot(first_rounded, up_weight)
    hidden = (jax.nn.silu(gate) * upward).astype(jnp.bfloat16)
    mixed = exact_dot(hidden, down_weight)
    return layer_norm(first_nodes + mixed, second_gain).astype(jnp.bfloat16)

def reference(node_query, query_angles, query_trans, query_chain, node_key, key_angles, key_trans, key_chain, pair_features, pair_mask, query_weight, key_weight, bias_weight, point_gain, chain_gain, out_weight, first_gain, second_gain, gate_weight, up_weight, down_weight, edge_query_weight, edge_key_weight, edge_in_weight, edge_out_weight):
    highest = lax.Precision.HIGHEST
    query_count = node_query.shape[0]
    key_count = node_key.shape[0]
    query_proj = exact_dot(node_query, query_weight).reshape(query_count, H, CH + 3 * PQ)
    query_vectors = rounded_copy(query_proj[:, :, :CH])
    query_points = jnp.einsum('abi,ihbp->ihap', rotations(query_angles), query_proj[:, :, CH:].reshape(query_count, H, 3, PQ), precision=highest) + query_trans.T[:, None, :, None]
    query_points = query_points.reshape(query_count, H, 3 * PQ)
    key_proj = exact_dot(node_key, key_weight).reshape(key_count, H, 2 * CH + 3 * PQ + 3 * PV)
    key_vectors = rounded_copy(key_proj[:, :, :CH])
    value_vectors = rounded_copy(key_proj[:, :, CH:2 * CH])
    key_frames = rotations(key_angles)
    key_points = jnp.einsum('abi,ihbp->ihap', key_frames, key_proj[:, :, 2 * CH:2 * CH + 3 * PQ].reshape(key_count, H, 3, PQ), precision=highest) + key_trans.T[:, None, :, None]
    key_points = key_points.reshape(key_count, H, 3 * PQ)
    value_points = jnp.einsum('abi,ihbp->ihap', key_frames, key_proj[:, :, 2 * CH + 3 * PQ:].reshape(key_count, H, 3, PV), precision=highest) + key_trans.T[:, None, :, None]
    value_points = value_points.reshape(key_count, H, 3 * PV)
    query_squares = lax.optimization_barrier(jnp.sum(query_points * query_points, axis=2)).T
    key_squares = lax.optimization_barrier(jnp.sum(key_points * key_points, axis=2)).T
    point_scale = point_gain * (math.sqrt(2.0 / (9.0 * PQ)) / 2.0)
    edge_keys = exact_dot(node_key, edge_key_weight)
    bias_float = bias_weight.astype(jnp.float32)
    edge_in_float = edge_in_weight.astype(jnp.float32)
    edge_out_float = edge_out_weight.astype(jnp.float32)
    block = math.gcd(query_count, 16)

    def one_block(index):
        begin = (index * block).astype(jnp.int32)

        def rows_of(values, axis):
            return lax.dynamic_slice_in_dim(values, begin, block, axis)
        tile = rows_of(pair_features, 1).astype(jnp.float32)
        bias = jnp.einsum('cij,ch->hij', tile, bias_float, precision=highest)
        inner = jnp.einsum('ihc,jhc->hij', rows_of(query_vectors, 0), key_vectors, precision=highest) / math.sqrt(CH)
        cross = jnp.einsum('ihd,jhd->hij', rows_of(query_points, 0), key_points, precision=highest)
        distance = rows_of(query_squares, 1)[:, :, None] + key_squares[:, None, :] - 2.0 * cross
        same_chain = (rows_of(query_chain, 0)[:, None] == key_chain[None, :]).astype(jnp.float32)
        scores = linear_scale * (inner + bias + chain_gain[:, None, None] * same_chain[None] - point_scale[:, None, None] * distance)
        scores = jnp.where(rows_of(pair_mask, 0)[None] == 1, scores, masked_score)
        row_max = lax.optimization_barrier(jnp.max(scores, axis=2))
        weights = jnp.exp(scores - row_max[:, :, None])
        totals = lax.optimization_barrier(jnp.sum(weights, axis=2))
        rounded_weights = rounded_copy(weights)
        vector_part = jnp.einsum('hij,jhc->ihc', rounded_weights, value_vectors, precision=highest)
        point_part = jnp.einsum('hij,jhd->ihd', weights, value_points, precision=highest)
        pair_part = jnp.einsum('hij,cij->ihc', rounded_weights, tile, precision=highest)
        attended = jnp.concatenate([vector_part, point_part, pair_part], axis=2) / totals.T[:, :, None]
        new_nodes = finish_nodes(attended, rows_of(node_query, 0), rows_of(query_angles, 1), rows_of(query_trans, 1), out_weight, first_gain, second_gain, gate_weight, up_weight, down_weight)
        edge_queries = exact_dot(new_nodes, edge_query_weight)
        edge_pre = jnp.einsum('cij,ce->eij', tile, edge_in_float, precision=highest) + edge_queries.T[:, :, None] + edge_keys.T[:, None, :]
        edge_hidden = rounded_copy(jnp.maximum(edge_pre, 0.0))
        edge_out = jnp.einsum('eij,ec->cij', edge_hidden, edge_out_float, precision=highest)
        return (new_nodes, (tile + edge_out).astype(jnp.bfloat16))
    nodes, pairs = lax.map(one_block, jnp.arange(query_count // block, dtype=jnp.int32))
    updated_nodes = nodes.reshape(query_count, CS)
    updated_pairs = jnp.moveaxis(pairs, 0, 1).reshape(CZ, query_count, key_count)
    return (updated_nodes, updated_pairs)
```

```python
import functools
import math

import jax
import jax.numpy as jnp
from jax import lax
from jax.experimental import pallas as pl
from jax.experimental.pallas import tpu as pltpu
from jax.sharding import PartitionSpec as P

CH = 16
PQ = 4
PV = 8

linear_scale = math.sqrt(1.0 / 3.0)
masked_score = -1000000000.0
norm_epsilon = 1e-05
ROWS = 16
SLOT = 16
DEPTH = 40
SMALL = CH + 4 * PV

MESH = pl.DeviceIdType.MESH
HIGH = lax.Precision.HIGHEST
F32 = jnp.float32
BF16 = jnp.bfloat16


def rotation_rows(angles):
    cy, sy = jnp.cos(angles[0:1]), jnp.sin(angles[0:1])
    cp, sp = jnp.cos(angles[1:2]), jnp.sin(angles[1:2])
    cr, sr = jnp.cos(angles[2:3]), jnp.sin(angles[2:3])
    return (
        (cy * cp, cy * sp * sr - sy * cr, cy * sp * cr + sy * sr),
        (sy * cp, sy * sp * sr + cy * cr, sy * sp * cr - cy * sr),
        (-sp, cp * sr, cp * cr),
    )


def layer_norm(values, gain):
    centred = values - jnp.mean(values, axis=-1, keepdims=True)
    variance = jnp.mean(centred * centred, axis=-1, keepdims=True)
    return centred * lax.rsqrt(variance + norm_epsilon) * gain


def dot(left, right, dims=(((1,), (0,)), ((), ())), precision=None):
    return lax.dot_general(left, right, dims, precision=precision, preferred_element_type=F32)


def take_rows(ref, rows):
    return jnp.concatenate([ref[t, rows, :] for t in range(ref.shape[0])], axis=1)


def put_rows(ref, rows, values):
    for t in range(ref.shape[0]):
        ref[t, rows, :] = values[:, t * 128 : (t + 1) * 128]


NT = (((1,), (1,)), ((), ()))
TN = (((0,), (0,)), ((), ()))


def kernel(
    dims,
    nq_ref, qa_ref, qt_ref, qc_ref, nk_ref, ka_ref, kt_ref, kc_ref, pair_ref, mask_ref,
    wq_ref, wk_ref, wb_ref, pg_ref, cg_ref, wo_ref, g1_ref, g2_ref,
    gate_hbm, up_hbm, down_hbm, weq_ref, wek_ref, wei_ref, weo_ref,
    nodes_ref, pairs_ref,
    xin, xown, keys, wq2, wk2, wb2, pg2, cg2, wo2, gate, up, down,
    padk, padq, padb, amat, bmat, vvec, vpts, ekt, lhs_in, lhs_out,
    xf, xt, sc_ref, pv_ref, s_ref, stat_send, stat_recv, fmat, lpmat, wsmall, wnorm, nq3,
    psend, precv, nsend, eqf, ostage, rstage,
    sem_in, sem_out, sem_own, key_s, key_r, w_s, w_r, ffn_sem, stat_s, stat_r,
    red_s, red_r, ag_s, ag_r, node_s, node_r, o_own, o_s, o_r,
):
    S, R, C, heads_local, half, kcount, share, channels = dims
    heads = heads_local * S
    blocks = half // ROWS
    s, row, col = lax.axis_index("sub"), lax.axis_index("row"), lax.axis_index("col")
    other = 1 - s

    barrier = pltpu.get_barrier_semaphore()
    group = [(dr, ds) for dr in range(R) for ds in range(S) if (dr, ds) != (0, 0)]

    def near(dr, ds):
        return {"row": lax.rem(row + dr, R), "sub": lax.rem(s + ds, S)}

    def along(dc):
        return {"col": lax.rem(col + dc, C)}

    for dr, ds in group:
        pl.semaphore_signal(barrier, inc=1, device_id=near(dr, ds), device_id_type=MESH)
    for dc in range(1, C):
        pl.semaphore_signal(barrier, inc=1, device_id=along(dc), device_id_type=MESH)
    pl.semaphore_wait(barrier, len(group) + C - 1)

    def remote(src, dst, send, recv, device):
        return pltpu.make_async_remote_copy(
            src_ref=src, dst_ref=dst, send_sem=send, recv_sem=recv,
            device_id=device, device_id_type=MESH,
        )

    key_copies = []
    for n, (dr, ds) in enumerate(group):
        copy = remote(nk_ref, keys.at[row * S + s], key_s.at[n], key_r.at[n], near(dr, ds))
        copy.start()
        key_copies.append(copy)
    weight_copies = []
    for n, (src, dst) in enumerate(
        ((wk_ref, wk2), (wq_ref, wq2), (wb_ref, wb2), (pg_ref, pg2), (cg_ref, cg2), (wo_ref, wo2))
    ):
        copy = remote(src, dst.at[s], w_s.at[n], w_r.at[n], {"sub": other})
        copy.start()
        weight_copies.append(copy)
    pair_copies = []
    own_copies = []
    for b in range(blocks):
        copy = remote(
            pair_ref.at[:, pl.ds(other * half + b * ROWS, ROWS), :],
            xin.at[b], sem_out.at[b], sem_in.at[b], {"sub": other},
        )
        copy.start()
        pair_copies.append(copy)
        copy = pltpu.make_async_copy(
            pair_ref.at[:, pl.ds(s * half + b * ROWS, ROWS), :], xown.at[b], sem_own.at[b]
        )
        copy.start()
        own_copies.append(copy)
    ffn_copies = []
    for n, (src, dst) in enumerate(((gate_hbm, gate), (up_hbm, up), (down_hbm, down))):
        copy = pltpu.make_async_copy(src, dst, ffn_sem.at[n])
        copy.start()
        ffn_copies.append(copy)
    keys[row * S + s] = nk_ref[...]
    wk2[s] = wk_ref[...]
    wq2[s] = wq_ref[...]
    wb2[s] = wb_ref[...]
    pg2[s] = pg_ref[...]
    cg2[s] = cg_ref[...]
    wo2[s] = wo_ref[...]

    kr = rotation_rows(ka_ref[...])
    kt = kt_ref[...]
    kcv = kc_ref[...]

    def pick(values):
        return jnp.where(s == 0, values[:, :half], values[:, half:])

    qr = rotation_rows(pick(qa_ref[...]))
    qt = pick(qt_ref[...])
    qcv = pick(qc_ref[...])

    for copy in weight_copies:
        copy.wait()
    for copy in key_copies:
        copy.wait()

    kall = keys[...].reshape(kcount, keys.shape[2])
    kwide = 2 * CH + 3 * PQ + 3 * PV
    qwide = CH + 3 * PQ
    point_scale = math.sqrt(2.0 / (9.0 * PQ)) / 2.0
    for hs in range(S):
        padk[:, : wk2.shape[2]] = dot(kall, wk2[hs])
        kp = padk[...].T
        padq[:, : wq2.shape[2]] = dot(nq_ref[...], wq2[hs])
        qp = pick(padq[...].T)
        for k in range(heads_local):
            h = hs * heads_local + k
            base = k * kwide
            bmat[h, 0:CH] = kp[base : base + CH].astype(BF16).astype(F32)
            vvec[h] = kp[base + CH : base + 2 * CH].astype(BF16)
            norm = jnp.zeros((1, kcount), F32)
            for a in range(3):
                g = kt[a : a + 1] + jnp.zeros((PQ, kcount), F32)
                v = kt[a : a + 1] + jnp.zeros((PV, kcount), F32)
                for b in range(3):
                    at = base + 2 * CH + b * PQ
                    g = g + kr[a][b] * kp[at : at + PQ]
                    at = base + 2 * CH + 3 * PQ + b * PV
                    v = v + kr[a][b] * kp[at : at + PV]
                bmat[h, CH + a * PQ : CH + a * PQ + PQ] = g
                vpts[h, a * PV : a * PV + PV] = v
                norm = norm + jnp.sum(g * g, axis=0, keepdims=True)
            top = CH + 3 * PQ
            bmat[h, top : top + 1] = jnp.ones((1, kcount), F32)
            bmat[h, top + 1 : top + 2] = norm
            for c in range(4):
                bmat[h, top + 2 + c : top + 3 + c] = (kcv == c).astype(F32)
            bmat[h, top + 6 :] = jnp.zeros((DEPTH - top - 6, kcount), F32)

            base = k * qwide
            gain = pg2[hs][:, k : k + 1] * (point_scale * linear_scale)
            chain = cg2[hs][:, k : k + 1] * linear_scale
            amat[h, 0:CH] = qp[base : base + CH].astype(BF16).astype(F32) * (
                linear_scale / math.sqrt(CH)
            )
            norm = jnp.zeros((1, half), F32)
            for a in range(3):
                g = qt[a : a + 1] + jnp.zeros((PQ, half), F32)
                for b in range(3):
                    at = base + CH + b * PQ
                    g = g + qr[a][b] * qp[at : at + PQ]
                amat[h, CH + a * PQ : CH + a * PQ + PQ] = g * (2.0 * gain)
                norm = norm + jnp.sum(g * g, axis=0, keepdims=True)
            amat[h, top : top + 1] = -gain * norm
            amat[h, top + 1 : top + 2] = -gain + jnp.zeros((1, half), F32)
            for c in range(4):
                amat[h, top + 2 + c : top + 3 + c] = jnp.where(qcv == c, chain, 0.0)
            amat[h, top + 6 :] = jnp.zeros((DEPTH - top - 6, half), F32)

    padb[...] = jnp.zeros(padb.shape, F32)
    for hs in range(S):
        padb[0:channels, hs * heads_local : (hs + 1) * heads_local] = wb2[hs].astype(F32)
    bias_left = (padb[...].T[0:SLOT] * linear_scale)
    bias_hi = bias_left.astype(BF16)
    bias_lo = (bias_left - bias_hi.astype(F32)).astype(BF16)
    bias_left = jnp.concatenate([bias_hi, bias_lo], axis=0)
    ekt[...] = dot(kall, wek_ref[...]).T
    lhs_in[:, 0:channels] = wei_ref[...].astype(F32).T.astype(BF16)
    lhs_out[...] = weo_ref[...].astype(F32).T.astype(BF16)

    cs = channels // S
    own_rows = pl.ds(pl.multiple_of(s * (cs * ROWS), cs * ROWS), cs * ROWS)
    other_rows = pl.ds(pl.multiple_of(other * (cs * ROWS), cs * ROWS), cs * ROWS)
    for b in range(blocks):
        own_copies[b].wait()
        pair_copies[b].wait()
        put_rows(xf, own_rows, xown[b].astype(F32).reshape(cs * ROWS, kcount))
        put_rows(xf, other_rows, xin[b].astype(F32).reshape(cs * ROWS, kcount))
        for i in range(ROWS):
            block = take_rows(xf, pl.ds(i, channels, stride=ROWS)).astype(BF16)
            xt[b * ROWS + i] = block
            both = dot(bias_left, block)
            at = (b * ROWS + i) * SLOT
            put_rows(sc_ref, pl.ds(at, SLOT), both[0:SLOT] + both[SLOT:])

    valid = mask_ref[pl.ds(pl.multiple_of(s * half, half), half), :] == 1
    lane = lax.broadcasted_iota(jnp.int32, (half, 128), 1)
    stats = jnp.zeros((half, 128), F32)
    for h in range(heads):
        scores = dot(amat[h], bmat[h], TN, HIGH)
        scores = scores + take_rows(sc_ref, pl.ds(h, half, stride=SLOT))
        scores = jnp.where(valid, scores, masked_score)
        top = jnp.max(scores, axis=1, keepdims=True)
        weights = jnp.exp(scores - top)
        total = jnp.sum(weights, axis=1, keepdims=True)
        rounded = weights.astype(BF16)
        put_rows(sc_ref, pl.ds(h, half, stride=SLOT), rounded.astype(F32))
        stats = jnp.where(lane == h, top, stats)
        stats = jnp.where(lane == SLOT + h, total, stats)
        pv_ref[h, 0:CH] = dot(vvec[h], rounded, NT)
        pv_ref[h, CH:] = dot(vpts[h], weights, NT, HIGH)
    padb[0:half] = stats
    stat_send[...] = padb[...].T[0 : 2 * SLOT]
    stat_copies = []
    for dc in range(1, C):
        copy = remote(stat_send, stat_recv.at[dc], stat_s.at[dc], stat_r.at[dc], along(dc))
        copy.start()
        stat_copies.append(copy)

    def pair_step(i, carry):
        at = pl.ds(pl.multiple_of(i * SLOT, SLOT), SLOT)
        s_ref[at, :] = dot(take_rows(sc_ref, at).astype(BF16), xt[i], NT)
        return carry

    lax.fori_loop(0, half, pair_step, 0)

    width = CH + 4 * PV + channels
    wnorm[...] = jnp.zeros(wnorm.shape, F32)
    for h in range(heads):
        hs, k = divmod(h, heads_local)
        wsmall[h * SMALL : (h + 1) * SMALL] = wo2[hs, k * width : k * width + SMALL]
        tail = wo2[hs, k * width + SMALL - 16 : k * width + SMALL].astype(F32)
        wnorm[h * PV : (h + 1) * PV] = tail[16 - PV :]
    nq = nq_ref[...].astype(F32)
    for k in range(S * C):
        nq3[k] = nq[k * share : (k + 1) * share]

    own_top, own_total = stat_send[0:SLOT, :], stat_send[SLOT:, :]
    for copy in stat_copies:
        copy.wait()
    all_top = own_top
    for dc in range(1, C):
        all_top = jnp.maximum(all_top, stat_recv[dc, 0:SLOT])
    all_total = own_total * jnp.exp(own_top - all_top)
    for dc in range(1, C):
        all_total = all_total + stat_recv[dc, SLOT:] * jnp.exp(stat_recv[dc, 0:SLOT] - all_top)
    live = lax.broadcasted_iota(jnp.int32, all_total.shape, 0) < heads
    factor = jnp.where(live, jnp.exp(own_top - all_top) / jnp.where(live, all_total, 1.0), 0.0)
    padb[...] = jnp.zeros(padb.shape, F32)
    padb[0:SLOT] = factor
    factor_columns = padb[...].T[0:half]

    fmat[...] = jnp.zeros(fmat.shape, F32)
    lpmat[...] = jnp.zeros(lpmat.shape, F32)
    for h in range(heads):
        f = factor[h : h + 1, 0:half]
        ft = f * own_total[h : h + 1, 0:half]
        at = h * SMALL
        fmat[at : at + CH, 0:half] = pv_ref[h, 0:CH] * f
        moved = []
        for a in range(3):
            p = pv_ref[h, CH + a * PV : CH + (a + 1) * PV]
            moved.append(p * f - qt[a : a + 1] * ft)
        for b in range(3):
            local = qr[0][b] * moved[0] + qr[1][b] * moved[1] + qr[2][b] * moved[2]
            fmat[at + CH + b * PV : at + CH + (b + 1) * PV, 0:half] = local
            lpmat[b * 128 + h * PV : b * 128 + (h + 1) * PV, 0:half] = local
    small = fmat[...].T[0:half, 0 : heads * SMALL].astype(BF16)
    projected = dot(small, wsmall[...])
    for h in range(heads):
        hs, k = divmod(h, heads_local)
        part = s_ref[pl.ds(h, half, stride=SLOT), :] * factor_columns[:, h : h + 1]
        projected = projected + dot(
            part.astype(BF16), wo2[hs, k * width + SMALL : (k + 1) * width]
        )
    points = lpmat[...].T[0:half]
    feat = projected.shape[1]
    for c in range(C):
        psend[c, :, 0:feat] = projected[c * share : (c + 1) * share].astype(BF16)
        psend[c, :, feat:] = points[c * share : (c + 1) * share].astype(BF16)
    red_copies = []
    for dc in range(1, C):
        copy = remote(
            psend.at[lax.rem(col + dc, C)], precv.at[dc], red_s.at[dc], red_r.at[dc], along(dc)
        )
        copy.start()
        red_copies.append(copy)
    for copy in ffn_copies:
        copy.wait()
    total = psend[col].astype(F32)
    for dc in range(1, C):
        red_copies[dc - 1].wait()
        total = total + precv[dc].astype(F32)
    x0, x1, x2 = total[:, feat : feat + 128], total[:, feat + 128 : feat + 256], total[:, feat + 256 :]
    norms = jnp.sqrt(1.0 + x0 * x0 + x1 * x1 + x2 * x2).astype(BF16)
    projected = total[:, 0:feat] + dot(norms, wnorm[...].astype(BF16))
    first = layer_norm(nq3[s * C + col] + projected, g1_ref[...])
    rounded = first.astype(BF16)
    gated = dot(rounded, gate[...])
    hidden = (gated / (1.0 + jnp.exp(-gated)) * dot(rounded, up[...])).astype(BF16)
    fresh = layer_norm(first + dot(hidden, down[...]), g2_ref[...]).astype(BF16)
    nsend[...] = fresh
    nodes_ref[s * C + col] = fresh
    ag_copies = []
    for dc in range(1, C):
        copy = remote(nsend, nodes_ref.at[s * C + col], ag_s.at[dc], ag_r.at[dc], along(dc))
        copy.start()
        ag_copies.append(copy)
    for copy in ag_copies:
        copy.wait()
    node_copy = remote(
        nodes_ref.at[pl.ds(s * C, C)], nodes_ref.at[pl.ds(s * C, C)],
        node_s.at[0], node_r.at[0], {"sub": other},
    )
    node_copy.start()
    eqf[...] = jnp.zeros(eqf.shape, F32)
    for c in range(C):
        eqf[c * share : (c + 1) * share] = dot(nodes_ref[s * C + c], weq_ref[...])
    eqt = eqf[...].T[:, 0:half]
    hi = eqt.astype(BF16)
    lo = (eqt - hi.astype(F32)).astype(BF16)
    lhs_in[:, channels : channels + 2 * half] = jnp.concatenate([hi, lo], axis=1)

    index = lax.broadcasted_iota(jnp.int32, (2 * half, kcount), 0)
    out_copies = []
    for b in range(blocks):
        for i in range(ROWS):
            block = xt[b * ROWS + i]
            at = b * ROWS + i
            mark = ((index == at) | (index == at + half)).astype(F32).astype(BF16)
            edge = dot(lhs_in[...], jnp.concatenate([block, mark], axis=0)) + ekt[...]
            edge = jnp.maximum(edge, 0.0).astype(BF16)
            put_rows(
                xf, pl.ds(i, channels, stride=ROWS), block.astype(F32) + dot(lhs_out[...], edge)
            )
        ostage[b] = take_rows(xf, own_rows).reshape(cs, ROWS, kcount).astype(BF16)
        rstage[b] = take_rows(xf, other_rows).reshape(cs, ROWS, kcount).astype(BF16)
        window = pairs_ref.at[:, pl.ds(s * half + b * ROWS, ROWS), :]
        copy = remote(rstage.at[b], window, o_s.at[b], o_r.at[b], {"sub": other})
        copy.start()
        out_copies.append(copy)
        copy = pltpu.make_async_copy(ostage.at[b], window, o_own.at[b])
        copy.start()
        out_copies.append(copy)
    for copy in out_copies:
        copy.wait()
    node_copy.wait()


def shards(
    node_query, query_angles, query_trans, query_chain, node_key, key_angles, key_trans,
    key_chain, pair_features, pair_mask, query_weight, key_weight, bias_weight, point_gain,
    chain_gain, out_weight, first_gain, second_gain, gate_weight, up_weight, down_weight,
    edge_query_weight, edge_key_weight, edge_in_weight, edge_out_weight,
):
    S, R, C = lax.axis_size("sub"), lax.axis_size("row"), lax.axis_size("col")
    qcount, features = node_query.shape
    kcount = key_angles.shape[1]
    half = qcount // S
    share = half // C
    cs = pair_features.shape[0]
    channels = cs * S
    heads_local = point_gain.shape[0]
    heads = heads_local * S
    blocks = half // ROWS
    hidden = edge_in_weight.shape[1]
    ffn = gate_weight.shape[1]
    kpad = -(-key_weight.shape[1] // 128) * 128
    qpad = -(-query_weight.shape[1] // 128) * 128
    small_rows = -(-heads * SMALL // 128) * 128
    group = R * S - 1
    dims = (S, R, C, heads_local, half, kcount, share, channels)
    vm = pl.BlockSpec(memory_space=pltpu.VMEM)
    anyspace = pl.BlockSpec(memory_space=pl.ANY)
    in_specs = [vm] * 8 + [anyspace] + [vm] * 9 + [anyspace] * 3 + [vm] * 4
    V = pltpu.VMEM
    DMA = pltpu.SemaphoreType.DMA
    scratch = [
        V((blocks, cs, ROWS, kcount), BF16),
        V((blocks, cs, ROWS, kcount), BF16),
        V((R * S, node_key.shape[0], features), BF16),
        V((S,) + query_weight.shape, BF16),
        V((S,) + key_weight.shape, BF16),
        V((S,) + bias_weight.shape, BF16),
        V((S, 1, heads_local), F32),
        V((S, 1, heads_local), F32),
        V((S,) + out_weight.shape, BF16),
        V(gate_weight.shape, BF16),
        V(up_weight.shape, BF16),
        V(down_weight.shape, BF16),
        V((kcount, kpad), F32),
        V((qcount, qpad), F32),
        V((128, 128), F32),
        V((heads, DEPTH, half), F32),
        V((heads, DEPTH, kcount), F32),
        V((heads, CH, kcount), BF16),
        V((heads, 3 * PV, kcount), F32),
        V((hidden, kcount), F32),
        V((hidden, channels + 2 * half), BF16),
        V((channels, hidden), BF16),
        V((kcount // 128, channels * ROWS, 128), F32),
        V((half, channels, kcount), BF16),
        V((kcount // 128, half * SLOT, 128), F32),
        V((heads, CH + 3 * PV, half), F32),
        V((half * SLOT, channels), F32),
        V((2 * SLOT, 128), F32),
        V((C, 2 * SLOT, 128), F32),
        V((small_rows, 128), F32),
        V((384, 128), F32),
        V((heads * SMALL, features), BF16),
        V((128, features), F32),
        V((S * C, share, features), F32),
        V((C, share, features + 384), BF16),
        V((C, share, features + 384), BF16),
        V((share, features), BF16),
        V((128, hidden), F32),
        V((blocks, cs, ROWS, kcount), BF16),
        V((blocks, cs, ROWS, kcount), BF16),
    ] + [
        DMA((n,))
        for n in (blocks, blocks, blocks, group, group, 6, 6, 3, C, C, C, C, C, C, 1, 1,
                  blocks, blocks, blocks)
    ]
    nodes, pairs = pl.pallas_call(
        functools.partial(kernel, dims),
        out_shape=(
            jax.ShapeDtypeStruct((S * C, share, features), BF16),
            jax.ShapeDtypeStruct(pair_features.shape, BF16),
        ),
        in_specs=in_specs,
        out_specs=(vm, anyspace),
        scratch_shapes=scratch,
        compiler_params=pltpu.CompilerParams(
            collective_id=0, has_side_effects=True, vmem_limit_bytes=60 * 1024 * 1024
        ),
    )(
        node_query, query_angles, query_trans, query_chain.reshape(1, qcount), node_key,
        key_angles, key_trans, key_chain.reshape(1, kcount), pair_features, pair_mask,
        query_weight, key_weight, bias_weight, point_gain.reshape(1, heads_local),
        chain_gain.reshape(1, heads_local), out_weight, first_gain.reshape(1, features),
        second_gain.reshape(1, features), gate_weight, up_weight, down_weight,
        edge_query_weight, edge_key_weight, edge_in_weight, edge_out_weight,
    )
    return nodes.reshape(qcount, features), pairs


def solution(mesh):
    return jax.shard_map(
        shards,
        mesh=mesh,
        in_specs=(
            P(("rep", "row"), None),
            P(None, ("rep", "row")),
            P(None, ("rep", "row")),
            P(("rep", "row")),
            P(("rep", "col", "row", "sub"), None),
            P(None, ("rep", "col")),
            P(None, ("rep", "col")),
            P(("rep", "col")),
            P("sub", ("rep", "row"), "col"),
            P(("rep", "row"), "col"),
            P(None, "sub"),
            P(None, "sub"),
            P(None, "sub"),
            P("sub"),
            P("sub"),
            P("sub", None),
            P(),
            P(),
            P(),
            P(),
            P(),
            P(),
            P(),
            P(),
            P(),
        ),
        out_specs=(P(("rep", "row"), None), P("sub", ("rep", "row"), "col")),
        check_vma=False,
    )
```
